32 devices in a mesh: ctx: 4 (over y, x), grp: 4 (over z), side: 2 (over core).
Axes of the slice: x: 2, y: 2, z: 4, core: 2. Of those that a mesh axis runs over, the one named last changes fastest.
Arguments:
- tokens: bfloat16 [512, 2048], P(('ctx', 'grp', 'side')), may hold values from -6 to 6
- norm_gain: float32 [2048], replicated, may hold values from 0.25 to 1.75
- combine: float32 [512, 8], P(('ctx', 'grp', 'side')), may hold values from 0.05 to 0.6
- expert_ids: int32 [512, 8], P(('ctx', 'grp', 'side')), may hold values from 0 to 15, all different within a row; in each aligned block of 16 rows (0 to 15, 16 to 31, ...) at most 11 rows name the same one
- w_gate: bfloat16 [16, 2048, 768], P(('ctx', 'grp'), None, 'side'), may hold values from -0.125 to 0.125
- w_up: bfloat16 [16, 2048, 768], P(('ctx', 'grp'), None, 'side'), may hold values from -0.125 to 0.125
- w_down: bfloat16 [16, 768, 2048], P(('ctx', 'grp'), 'side'), may hold values from -0.21875 to 0.21875
- d_out: bfloat16 [512, 2048], P(('ctx', 'grp', 'side')), may hold values from -6 to 6
Outputs:
- mixed: bfloat16 [512, 2048], P(('ctx', 'grp', 'side'))
- d_tokens: bfloat16 [512, 2048], P(('ctx', 'grp', 'side'))
- d_gain: float32 [2048], replicated
- d_combine: float32 [512, 8], P(('ctx', 'grp', 'side'))
- d_w_gate: bfloat16 [16, 2048, 768], P(('ctx', 'grp'), None, 'side')
- d_w_up: bfloat16 [16, 2048, 768], P(('ctx', 'grp'), None, 'side')
- d_w_down: bfloat16 [16, 768, 2048], P(('ctx', 'grp'), 'side')
The draws below stay inside these ranges and needn't reach their ends.
Inputs may be any that keep to these rules, and one draw needn't show every extreme that they name: `expert_ids`: each row names 8 different experts; among the 16 rows of one device no expert is named more than 11 times, and that bound is reached.
All inputs are finite; a program needn't handle non-finite values.
Results may differ from the reference program's by a relative error of at most 0.0072.
Values may be sent and summed in bfloat16 or wider, within the bound.
A program may use at most 128 MiB of HBM per device.

```python
import math
import jax
import jax.numpy as jnp
import numpy as np
from jax import lax

D = 2048
FF = 768
TOP = 8
TOK_DEV = 16
EXPERTS = 16
TOKENS = 512
SLOTS = 11


def steps_of(stream_key, dims, cuts, low, top_value):
    def one(axis_at, parts):
        steps = jax.random.uniform(jax.random.fold_in(jax.random.fold_in(stream_key, 6), axis_at), (parts,), jnp.float32, low / len(cuts), top_value / len(cuts))
        return jnp.repeat(jnp.exp(steps), dims[axis_at] // parts).reshape((-1,) + (1,) * (len(dims) - axis_at - 1))

    factor_of = one(*cuts[0])
    for cut in cuts[1:]:
        factor_of = factor_of * one(*cut)
    return factor_of


def assign_block(key, own, number, rows, number_of, top, bound, skew):
    order = jax.random.permutation(key, number_of)
    heavy_load, ordinary = load_shares(number_of, rows * top, bound, skew, True), load_shares(number_of, rows * top, bound, skew, False)
    places = jnp.arange(number_of)

    def named(sizes, rotation):
        used = int((sizes > 0).sum())
        fixed = max(1, used // 4)
        shifted = fixed + (places - fixed + rotation * (used - fixed)) % max(1, number_of - fixed)
        return jnp.zeros((number_of,), jnp.int32).at[order[jnp.where(places < fixed, places, shifted)]].set(jnp.asarray(sizes, jnp.int32))

    sizes = jnp.where(number % 4 == 0, named(heavy_load, number // 4), named(ordinary, number - number // 4 - 1))
    mixed = jax.random.permutation(jax.random.fold_in(own, 3), number_of)
    giver, sink = mixed[0:number_of // 2 * 2:2], mixed[1:number_of // 2 * 2:2]
    room = jnp.minimum(sizes[giver] - 1, bound - sizes[sink]) // 2
    room = jnp.where((giver == order[0]) | (sink == order[0]) | (sizes[sink] == 0), 0, jnp.maximum(room, 0))
    shifted = jax.random.randint(jax.random.fold_in(own, 4), (number_of // 2,), 0, 1 << 20) % (room + 1)
    sizes = sizes.at[giver].add(-shifted).at[sink].add(shifted)
    members = jnp.searchsorted(jnp.cumsum(sizes), jnp.arange(rows * top), side="right").astype(jnp.int32)
    table = members.reshape(top, rows).T
    table = table[jax.random.permutation(jax.random.fold_in(own, 1), rows)]
    rotation = jax.random.randint(jax.random.fold_in(own, 2), (rows, 1), 0, top)
    return jnp.take_along_axis(table, (jnp.arange(top)[None, :] + rotation) % top, axis=1)


def load_shares(amount, total, limit, lean, full):
    loads = [(1 << 20) // math.isqrt(rank ** lean) + 1 for rank in range(1, amount + 1)]
    largest = limit if full else min(limit, max(-(-total // amount), total * loads[0] // sum(loads)))
    least = 1 if total - largest >= amount - 1 else 0
    counts, spare = [largest] + [least] * (amount - 1), total - largest - least * (amount - 1)
    while spare > 0:
        movable = [i for i in range(1, amount) if counts[i] < largest] or [i for i in range(1, amount) if counts[i] < limit]
        mass, left = sum([loads[i] for i in movable]), spare
        for i in movable:
            extra = min(limit - counts[i], max(1, left * loads[i] // mass), spare)
            counts[i] = counts[i] + extra
            spare = spare - extra
    return np.array(counts)


def gaussian(own_key, shape, spread, reach, split=(), kind=jnp.bfloat16):
    result = spread * jax.random.normal(own_key, shape, jnp.float32)
    if split:
        result = result * steps_of(own_key, shape, split, -0.22, 0.18)
    return jnp.clip(result, -reach, reach).astype(kind)


def setup_inputs(seed: int = 0) -> dict:
    key_list = jax.random.split(jax.random.key(seed), 9)
    tokens = gaussian(key_list[0], (TOKENS, D), 1.0, 6.0, ((0, 32),))
    norm_gain = jnp.clip(1.0 + 0.15 * jax.random.normal(key_list[1], (D,), jnp.float32), 0.25, 1.75)
    combine = jnp.clip(jnp.exp(math.log(0.6) - 2.4849067 * jax.random.uniform(key_list[2], (TOKENS, TOP), jnp.float32) ** steps_of(key_list[2], (TOKENS, TOP), ((0, 32),), -0.2, 0.2)), 0.05, 0.6)
    expert_ids_keys = jax.random.split(jax.random.fold_in(key_list[3], 1), TOKENS // TOK_DEV)
    expert_ids_turns = jax.random.permutation(jax.random.fold_in(key_list[3], 3), TOKENS // TOK_DEV)
    expert_ids = jax.vmap(lambda own, number: assign_block(jax.random.fold_in(key_list[3], 2), own, number, TOK_DEV, EXPERTS, TOP, SLOTS, 2))(expert_ids_keys, expert_ids_turns).reshape((TOKENS, TOP))
    w_gate = gaussian(key_list[4], (EXPERTS, D, FF), D ** -0.5, 0.125, ((0, 16), (2, 2)))
    w_up = gaussian(key_list[5], (EXPERTS, D, FF), D ** -0.5, 0.125, ((0, 16), (2, 2)))
    w_down = gaussian(key_list[6], (EXPERTS, FF, D), FF ** -0.5, 0.21875, ((0, 16), (1, 2)))
    d_out = gaussian(key_list[7], (TOKENS, D), 1.0, 6.0, ((0, 32),))
    return dict(tokens=tokens, norm_gain=norm_gain, combine=combine, expert_ids=expert_ids, w_gate=w_gate, w_up=w_up, w_down=w_down, d_out=d_out)


EPS = 1e-06

def expert_pass(rows, grads, gate_w, up_w, down_w):
    a_gate = jnp.dot(rows, gate_w, preferred_element_type=jnp.float32)
    a_up = jnp.dot(rows, up_w, preferred_element_type=jnp.float32)
    sigmoid_gate = jax.nn.sigmoid(a_gate)
    silu_gate = a_gate * sigmoid_gate
    hidden = (silu_gate * a_up).astype(jnp.bfloat16)
    output = jnp.dot(hidden, down_w, preferred_element_type=jnp.float32)
    d_hidden = lax.dot_general(grads, down_w, (((1,), (1,)), ((), ())), preferred_element_type=jnp.float32)
    d_up = (d_hidden * silu_gate).astype(jnp.bfloat16)
    d_gate = (d_hidden * a_up * sigmoid_gate * (1.0 + a_gate * (1.0 - sigmoid_gate))).astype(jnp.bfloat16)
    d_rows = lax.dot_general(d_gate, gate_w, (((1,), (1,)), ((), ())), preferred_element_type=jnp.float32)
    d_rows = d_rows + lax.dot_general(d_up, up_w, (((1,), (1,)), ((), ())), preferred_element_type=jnp.float32)
    g_gate = lax.dot_general(rows, d_gate, (((0,), (0,)), ((), ())), preferred_element_type=jnp.float32)
    g_up = lax.dot_general(rows, d_up, (((0,), (0,)), ((), ())), preferred_element_type=jnp.float32)
    g_down = lax.dot_general(hidden, grads, (((0,), (0,)), ((), ())), preferred_element_type=jnp.float32)
    return (output, d_rows, g_gate, g_up, g_down)

def row_table(expert_ids):
    blocks = TOKENS // TOK_DEV
    flat_ids = expert_ids.reshape(blocks, TOK_DEV * TOP).astype(jnp.int32)
    onehot = (flat_ids[:, :, None] == jnp.arange(EXPERTS, dtype=jnp.int32)[None, None, :]).astype(jnp.int32)
    before = jnp.cumsum(onehot, axis=1) - onehot
    slot = lax.optimization_barrier(jnp.sum(before * onehot, axis=2)).astype(jnp.int32)
    block_ids = jnp.arange(blocks, dtype=jnp.int32)[:, None]
    target = flat_ids * (blocks * SLOTS) + block_ids * SLOTS + slot
    return target.reshape(-1).astype(jnp.int32)

def reference(tokens, norm_gain, combine, expert_ids, w_gate, w_up, w_down, d_out):
    x_float = tokens.astype(jnp.float32)
    inv_rms = lax.rsqrt(lax.optimization_barrier(jnp.mean(x_float * x_float, axis=1, keepdims=True)) + EPS)
    normed = (x_float * inv_rms * norm_gain).astype(jnp.bfloat16)
    grad_float = d_out.astype(jnp.float32)
    d_slot = (combine[:, :, None] * grad_float[:, None, :]).astype(jnp.bfloat16)
    target = row_table(expert_ids)
    per_expert = TOKENS // TOK_DEV * SLOTS
    total = EXPERTS * per_expert
    rows_in = jnp.zeros((total, D), jnp.bfloat16).at[target].set(jnp.repeat(normed, TOP, axis=0))
    grads_in = jnp.zeros((total, D), jnp.bfloat16).at[target].set(d_slot.reshape(TOKENS * TOP, D))

    def one_expert(operands):
        rows, grads, gate_w, up_w, down_w = operands
        output, d_rows, g_gate, g_up, g_down = expert_pass(rows, grads, gate_w, up_w, down_w)
        return (output.astype(jnp.bfloat16), d_rows.astype(jnp.bfloat16), g_gate.astype(jnp.bfloat16), g_up.astype(jnp.bfloat16), g_down.astype(jnp.bfloat16))
    expert_out, expert_back, d_w_gate, d_w_up, d_w_down = lax.map(one_expert, (rows_in.reshape(EXPERTS, per_expert, D), grads_in.reshape(EXPERTS, per_expert, D), w_gate, w_up, w_down))
    slot_out = expert_out.reshape(total, D)[target].astype(jnp.float32).reshape(TOKENS, TOP, D)
    slot_back = expert_back.reshape(total, D)[target].astype(jnp.float32).reshape(TOKENS, TOP, D)
    mixed = (x_float + lax.optimization_barrier(jnp.sum(combine[:, :, None] * slot_out, axis=1))).astype(jnp.bfloat16)
    d_combine = jnp.einsum('tkd,td->tk', slot_out, grad_float, precision=lax.Precision.HIGHEST)
    d_normed = lax.optimization_barrier(jnp.sum(slot_back, axis=1))
    d_gain = lax.optimization_barrier(jnp.sum(d_normed * x_float * inv_rms, axis=0))
    scaled = d_normed * norm_gain
    d_tokens = grad_float + inv_rms * scaled - x_float * inv_rms ** 3 * lax.optimization_barrier(jnp.mean(scaled * x_float, axis=1, keepdims=True))
    return (mixed, d_tokens.astype(jnp.bfloat16), d_gain, d_combine, d_w_gate, d_w_up, d_w_down)
```

```python
import jax
import jax.numpy as jnp
from jax import lax
from jax.experimental import pallas as pl
from jax.experimental.pallas import tpu as pltpu
from jax.sharding import PartitionSpec as P

EPS = 1e-06


def expert_pass(rows, grads, gate_w, up_w, down_w):
    a_gate = jnp.dot(rows, gate_w, preferred_element_type=jnp.float32)
    a_up = jnp.dot(rows, up_w, preferred_element_type=jnp.float32)
    sigmoid_gate = jax.nn.sigmoid(a_gate)
    silu_gate = a_gate * sigmoid_gate
    hidden = (silu_gate * a_up).astype(jnp.bfloat16)
    output = jnp.dot(hidden, down_w, preferred_element_type=jnp.float32)
    d_hidden = lax.dot_general(
        grads, down_w, (((1,), (1,)), ((), ())), preferred_element_type=jnp.float32
    )
    d_up = (d_hidden * silu_gate).astype(jnp.bfloat16)
    d_gate = (d_hidden * a_up * sigmoid_gate * (1.0 + a_gate * (1.0 - sigmoid_gate))).astype(
        jnp.bfloat16
    )
    d_rows = lax.dot_general(
        d_gate, gate_w, (((1,), (1,)), ((), ())), preferred_element_type=jnp.float32
    )
    d_rows = d_rows + lax.dot_general(
        d_up, up_w, (((1,), (1,)), ((), ())), preferred_element_type=jnp.float32
    )
    g_gate = lax.dot_general(
        rows, d_gate, (((0,), (0,)), ((), ())), preferred_element_type=jnp.float32
    )
    g_up = lax.dot_general(rows, d_up, (((0,), (0,)), ((), ())), preferred_element_type=jnp.float32)
    g_down = lax.dot_general(
        hidden, grads, (((0,), (0,)), ((), ())), preferred_element_type=jnp.float32
    )
    return (output, d_rows, g_gate, g_up, g_down)


def local(tokens, norm_gain, combine, expert_ids, w_gate, w_up, w_down, d_out):
    count = tokens.shape[0]
    width = tokens.shape[1]
    chosen = expert_ids.shape[1]
    n_ctx = lax.axis_size("ctx")
    n_grp = lax.axis_size("grp")
    experts = n_ctx * n_grp
    slots = max(2, (4 * count * chosen + 3 * experts - 1) // (3 * experts))
    places = experts * slots
    x_float = tokens.astype(jnp.float32)
    inv_rms = lax.rsqrt(jnp.mean(x_float * x_float, axis=1, keepdims=True) + EPS)
    normed = (x_float * inv_rms * norm_gain).astype(jnp.bfloat16)
    grad_float = d_out.astype(jnp.float32)
    flat_ids = expert_ids.reshape(-1)
    onehot = (flat_ids[:, None] == jnp.arange(experts, dtype=jnp.int32)[None, :]).astype(jnp.int32)
    before = jnp.cumsum(onehot, axis=0) - onehot
    slot = jnp.sum(before * onehot, axis=1)
    target = flat_ids * slots + slot
    select = (target[:, None] == jnp.arange(places, dtype=jnp.int32)[None, :]).astype(jnp.float32)
    per_token = select.reshape(count, chosen, places)
    token_map = jnp.sum(per_token, axis=1).astype(jnp.bfloat16)
    weighted = jnp.sum(per_token * combine[:, :, None], axis=1)
    send_rows = lax.dot_general(
        token_map, normed, (((0,), (0,)), ((), ())), preferred_element_type=jnp.float32
    ).astype(jnp.bfloat16)
    send_grads = lax.dot_general(
        weighted,
        grad_float,
        (((0,), (0,)), ((), ())),
        precision=lax.Precision.HIGHEST,
        preferred_element_type=jnp.float32,
    ).astype(jnp.bfloat16)
    rows_in, grads_in = (
        lax.all_to_all(
            send_rows.reshape(experts, slots, width),
            ("ctx", "grp"),
            split_axis=0,
            concat_axis=0,
            tiled=True,
        ),
        lax.all_to_all(
            send_grads.reshape(experts, slots, width),
            ("ctx", "grp"),
            split_axis=0,
            concat_axis=0,
            tiled=True,
        ),
    )
    full_gate, full_up, full_down = (
        lax.all_gather(w_gate[0], "side", axis=1, tiled=True),
        lax.all_gather(w_up[0], "side", axis=1, tiled=True),
        lax.all_gather(w_down[0], "side", axis=0, tiled=True),
    )
    output, d_rows, g_gate, g_up, g_down = expert_pass(
        rows_in.reshape(places, width),
        grads_in.reshape(places, width),
        full_gate,
        full_up,
        full_down,
    )
    own_gate, own_up, own_down = (
        lax.psum_scatter(g_gate, "side", scatter_dimension=1, tiled=True),
        lax.psum_scatter(g_up, "side", scatter_dimension=1, tiled=True),
        lax.psum_scatter(g_down, "side", scatter_dimension=0, tiled=True),
    )
    back_out = output.astype(jnp.bfloat16)
    back_rows = d_rows.astype(jnp.bfloat16)
    came_out, came_rows = (
        lax.all_to_all(
            back_out.reshape(experts, slots, width),
            ("ctx", "grp"),
            split_axis=0,
            concat_axis=0,
            tiled=True,
        ),
        lax.all_to_all(
            back_rows.reshape(experts, slots, width),
            ("ctx", "grp"),
            split_axis=0,
            concat_axis=0,
            tiled=True,
        ),
    )
    slot_out = jnp.dot(
        select.astype(jnp.bfloat16),
        came_out.reshape(places, width),
        preferred_element_type=jnp.float32,
    ).reshape(count, chosen, width)
    mixed = (x_float + jnp.sum(combine[:, :, None] * slot_out, axis=1)).astype(jnp.bfloat16)
    d_combine = jnp.einsum("tkd,td->tk", slot_out, grad_float, precision=lax.Precision.HIGHEST)
    d_normed = jnp.dot(
        token_map, came_rows.reshape(places, width), preferred_element_type=jnp.float32
    )
    d_gain = lax.psum(jnp.sum(d_normed * x_float * inv_rms, axis=0), ("ctx", "grp", "side"))
    scaled = d_normed * norm_gain
    d_tokens = (
        grad_float
        + inv_rms * scaled
        - x_float * inv_rms**3 * jnp.mean(scaled * x_float, axis=1, keepdims=True)
    )
    return (
        mixed,
        d_tokens.astype(jnp.bfloat16),
        d_gain,
        d_combine,
        own_gate.astype(jnp.bfloat16)[None],
        own_up.astype(jnp.bfloat16)[None],
        own_down.astype(jnp.bfloat16)[None],
    )


MESH = pl.DeviceIdType.MESH
LANES = 128


def fits(mesh):
    return mesh.shape["ctx"] == 4 and mesh.shape["side"] == 2 and mesh.shape["grp"] <= 4


def kernel(
    n_grp,
    tok_ref, gain_ref, comb_ref, ids_ref, wg_hbm, wu_hbm, wd_hbm, dout_ref,
    mixed_ref, dtok_ref, dgain_ref, dcomb_ref, gg_hbm, gu_hbm, gd_hbm,
    xg, dg, wg, wu, wd, cw, mo, bo, rs, rp1, rp2, rz, dgb, act, gwg, gwu, gwd, acc,
    zs_s, zs_r, p1_s, p1_r, p2_s, p2_r, sd_s, sd_r,
    rs_s, rs_r, q1_s, q1_r, q2_s, q2_r, rz_s, rz_r, dg_s, dg_r, w_sem, o_sem,
):
    G = n_grp
    count, width = tok_ref.shape
    full = xg.shape[2]
    half = wg.shape[1]
    chunks = xg.shape[0]
    total = chunks * count
    c, g, s = lax.axis_index("ctx"), lax.axis_index("grp"), lax.axis_index("side")
    x, y = c % 2, c // 2
    cx, cy, cxy = y * 2 + (1 - x), (1 - y) * 2 + x, (1 - y) * 2 + (1 - x)
    o = 1 - s
    expert = c * G + g
    bf, f32 = jnp.bfloat16, jnp.float32

    def idx(cc, gg, ss):
        return (cc * G + gg) * 2 + ss

    def rc(src, dst, ssem, rsem, dev):
        return pltpu.make_async_remote_copy(
            src_ref=src, dst_ref=dst, send_sem=ssem, recv_sem=rsem, device_id=dev, device_id_type=MESH
        )

    loads = [
        pltpu.make_async_copy(a.at[0], b, w_sem.at[i])
        for i, (a, b) in enumerate(((wg_hbm, wg), (wu_hbm, wu), (wd_hbm, wd)))
    ]

    barrier = pltpu.get_barrier_semaphore()
    peers = [(cx, g, s), (cy, g, s), (c, g, o)] + [(c, (g + k) % G, s) for k in range(1, G)]
    for dev in peers:
        pl.semaphore_signal(barrier, inc=1, device_id=dev, device_id_type=MESH)

    x_f = tok_ref[...].astype(f32)
    inv = lax.rsqrt(jnp.mean(x_f * x_f, axis=1, keepdims=True) + EPS)
    lane = lax.broadcasted_iota(jnp.int32, (count, LANES), 1)
    table = jnp.zeros((count, LANES), f32)
    ids = ids_ref[...]
    comb = comb_ref[...]
    chosen = ids.shape[1]
    for k in range(chosen):
        table += jnp.where(lane == ids[:, k : k + 1], comb[:, k : k + 1], 0.0)
    high = table.astype(bf)
    me = idx(c, g, s)
    xg[me, :, :width] = (x_f * inv * gain_ref[...]).astype(bf)
    xg[me, :, width:] = high
    dg[me, :, :width] = dout_ref[...]
    dg[me, :, width:] = (table - high.astype(f32)).astype(bf)

    pl.semaphore_wait(barrier, len(peers))

    arrays = (xg, dg)
    first, second = (cx, cy), (cy, cx)
    offs = [0]
    for k in range(1, G):
        offs += [k, -k]

    def z_copy(a, gg, up):
        i = idx(c, gg, s)
        to = g + 1 if up else g - 1
        return rc(arrays[a].at[i], arrays[a].at[i], zs_s.at[a, int(up), gg], zs_r.at[a, gg], (c, to, s))

    def p1_copy(a, gg, cc):
        i = idx(cc, gg, s)
        return rc(arrays[a].at[i], arrays[a].at[i], p1_s.at[a, gg], p1_r.at[a, gg], (first[a], g, s))

    def p2_copy(a, j, gg, cc):
        i = idx(cc, gg, s)
        return rc(arrays[a].at[i], arrays[a].at[i], p2_s.at[a, j, gg], p2_r.at[a, j, gg], (second[a], g, s))

    def side_copy(a, gg, cc, ss):
        i = idx(cc, gg, ss)
        return rc(arrays[a].at[i], arrays[a].at[i], sd_s.at[a, cc, gg], sd_r.at[a, cc, gg], (c, g, o))

    def inside(gg):
        return jnp.logical_and(gg >= 0, gg < G)

    for off in offs:
        gg = g + off

        @pl.when(inside(gg))
        def _(gg=gg, off=off):
            for a in (0, 1):
                if off != 0:
                    z_copy(a, gg, off < 0).wait_recv()
                if off >= 0:
                    @pl.when(g > 0)
                    def _():
                        z_copy(a, gg, False).start()
                if off <= 0:
                    @pl.when(g < G - 1)
                    def _():
                        z_copy(a, gg, True).start()
                p1_copy(a, gg, c).start()
                p2_copy(a, 0, gg, c).start()
                side_copy(a, gg, c, s).start()

    for load in loads:
        load.start()

    for off in offs:
        gg = g + off

        @pl.when(inside(gg))
        def _(gg=gg):
            for a in (0, 1):
                p1_copy(a, gg, first[a]).wait_recv()
                p2_copy(a, 1, gg, first[a]).start()
                side_copy(a, gg, first[a], s).start()

    for off in offs:
        gg = g + off

        @pl.when(inside(gg))
        def _(gg=gg):
            for a in (0, 1):
                p2_copy(a, 0, gg, second[a]).wait_recv()
                side_copy(a, gg, second[a], s).start()
            for a in (0, 1):
                p2_copy(a, 1, gg, cxy).wait_recv()
                side_copy(a, gg, cxy, s).start()

    for cc in range(4):
        for gg in range(G):
            for a in (0, 1):
                side_copy(a, gg, cc, o).wait_recv()
    for load in loads:
        load.wait()

    rows = total // 2
    mine = (lax.broadcasted_iota(jnp.int32, (rows, LANES), 1) == expert).astype(f32)
    nt = (((1,), (1,)), ((), ()))
    tn = (((0,), (0,)), ((), ()))
    ch = chunks // 2

    def forward(i, gain_sum):
        b = (i + 1 - y) % 2
        part = pl.ds(b * ch, ch)
        at = pl.ds(pl.multiple_of(b * rows, rows), rows)
        xr = xg[part, :, :width].reshape(rows, width)
        dr = dg[part, :, :width].reshape(rows, width)
        weight = xg[part, :, width:].astype(f32).reshape(rows, LANES)
        weight = weight + dg[part, :, width:].astype(f32).reshape(rows, LANES)
        weight = jnp.sum(weight * mine, axis=1, keepdims=True)
        a_gate = jnp.dot(xr, wg[...], preferred_element_type=f32)
        a_up = jnp.dot(xr, wu[...], preferred_element_type=f32)
        raw = lax.dot_general(dr, wd[...], nt, preferred_element_type=f32)
        sig = jax.nn.sigmoid(a_gate)
        silu = a_gate * sig
        hidden = silu * a_up
        dc = jnp.sum(hidden * raw, axis=1, keepdims=True)
        d_hidden = raw * weight
        hc = (hidden * weight).astype(bf)
        d_up = (d_hidden * silu).astype(bf)
        d_gate = (d_hidden * a_up * sig * (1.0 + a_gate * (1.0 - sig))).astype(bf)
        act[0, at, :] = d_gate
        act[1, at, :] = d_up
        act[2, at, :] = hc
        dcol = jnp.where(weight > 0.0, dc, 0.0) * mine
        mo[part, :, width:] = dcol.astype(bf).reshape(ch, count, LANES)
        out = jnp.dot(hc, wd[...], preferred_element_type=f32)
        mo[part, :, :width] = out.astype(bf).reshape(ch, count, width)
        back = lax.dot_general(d_gate, wg[...], nt, preferred_element_type=f32)
        back += lax.dot_general(d_up, wu[...], nt, preferred_element_type=f32)
        bo[part, :, :] = back.astype(bf).reshape(ch, count, width)
        gain_sum = gain_sum + jnp.sum(back * xr.astype(f32), axis=0, keepdims=True)

        for k in range(2):
            cc = 2 * b + k
            for gg in range(G):
                for a in (0, 1):
                    rs_copy(a, cc, gg, o).start()
        return gain_sum

    outs = (mo, bo)
    wide = (full, width)

    def rs_copy(a, cc, gg, ss):
        return rc(
            outs[a].at[idx(cc, gg, ss)], rs.at[a, cc * G + gg, :, : wide[a]],
            rs_s.at[a, cc, gg], rs_r.at[a, cc, gg], (c, g, o),
        )

    n1, n2 = (cy, cx), (cx, cy)

    def q1_copy(a, j, gg, cc):
        return rc(
            outs[a].at[idx(cc, gg, s)], rp1.at[a, j, gg, :, : wide[a]],
            q1_s.at[a, j, gg], q1_r.at[a, j, gg], (n1[a], g, s),
        )

    def q2_copy(a, gg, cc):
        return rc(
            outs[a].at[idx(cc, gg, s)], rp2.at[a, gg, :, : wide[a]],
            q2_s.at[a, gg], q2_r.at[a, gg], (n2[a], g, s),
        )

    def rz_copy(a, up, gg):
        to = g + 1 if up else g - 1
        return rc(
            outs[a].at[idx(c, gg, s)], rz.at[a, int(up), gg, :, : wide[a]],
            rz_s.at[a, int(up), gg], rz_r.at[a, int(up), gg], (c, to, s),
        )

    def add(a, cc, gg, terms):
        i = idx(cc, gg, s)
        value = outs[a][i].astype(f32)
        for term in terms:
            value = value + term[:, : wide[a]].astype(f32)
        outs[a][i] = value.astype(bf)

    gain_sum = lax.fori_loop(0, 2, forward, jnp.zeros((1, width), f32))
    dgb[0] = gain_sum / gain_ref[...]

    gain_devs = [(c, g, o), (cx, g, s), (cy, g, s)]

    def dg_copy(k):
        return rc(dgb.at[k], dgb.at[8 + k], dg_s.at[k], dg_r.at[k], gain_devs[k])

    def dgz_copy(k):
        return rc(dgb.at[3], dgb.at[8 + 2 + k], dg_s.at[2 + k], dg_r.at[2 + k], (c, (g + k) % G, s))

    dg_copy(0).start()

    order = [(g + G // 2 + i) % G for i in range(G)]
    for j in (1, 0):
        for gg in order:
            for a in (0, 1):
                cc = cxy if j else n1[a]
                rs_copy(a, cc, gg, s).wait_recv()
                add(a, cc, gg, [rs[a, cc * G + gg]])
                q1_copy(a, j, gg, cc).start()

    dg_copy(0).wait_recv()
    dgb[1] = dgb[0] + dgb[8]
    dg_copy(1).start()

    blk = width // 4

    def grads(i, carry):
        cols = pl.ds(pl.multiple_of(i * blk, blk), blk)
        xr = xg[:, :, cols].reshape(total, blk)
        dr = dg[:, :, cols].reshape(total, blk)
        gwg[cols, :] = lax.dot_general(xr, act[0], tn, preferred_element_type=f32).astype(bf)
        gwu[cols, :] = lax.dot_general(xr, act[1], tn, preferred_element_type=f32).astype(bf)
        gwd[:, cols] = lax.dot_general(act[2], dr, tn, preferred_element_type=f32).astype(bf)
        return carry

    lax.fori_loop(0, 4, grads, 0)
    stores = [
        pltpu.make_async_copy(b, a.at[0], o_sem.at[i])
        for i, (a, b) in enumerate(((gg_hbm, gwg), (gu_hbm, gwu), (gd_hbm, gwd)))
    ]
    for store in stores:
        store.start()

    dg_copy(1).wait_recv()
    dgb[2] = dgb[1] + dgb[9]
    dg_copy(2).start()

    for gg in order:
        for a in (0, 1):
            rs_copy(a, n2[a], gg, s).wait_recv()
            q1_copy(a, 1, gg, cxy).wait_recv()
            add(a, n2[a], gg, [rs[a, n2[a] * G + gg], rp1[a, 1, gg]])
            q2_copy(a, gg, n2[a]).start()

    dg_copy(2).wait_recv()
    dgb[3] = dgb[2] + dgb[10]
    for k in range(1, G):
        dgz_copy(k).start()

    for gg in order:
        for a in (0, 1):
            rs_copy(a, c, gg, s).wait_recv()
            q1_copy(a, 0, gg, c).wait_recv()
            q2_copy(a, gg, c).wait_recv()
            add(a, c, gg, [rs[a, c * G + gg], rp1[a, 0, gg], rp2[a, gg]])

    for k in range(G - 1, 0, -1):
        for up in (True, False):
            gg = g + k if up else g - k

            @pl.when(inside(gg))
            def _(gg=gg, up=up):
                for a in (0, 1):
                    @pl.when(g > 0 if up else g < G - 1)
                    def _():
                        rz_copy(a, up, gg).wait_recv()
                        add(a, c, gg, [rz[a, int(up), gg]])

                    rz_copy(a, up, gg).start()

    for a in (0, 1):
        acc[a, :, : wide[a]] = outs[a][me].astype(f32)
        for up in (True, False):
            @pl.when(g > 0 if up else g < G - 1)
            def _():
                rz_copy(a, up, g).wait_recv()
                acc[a, :, : wide[a]] += rz[a, int(up), g, :, : wide[a]].astype(f32)

    x_f = tok_ref[...].astype(f32)
    inv = lax.rsqrt(jnp.mean(x_f * x_f, axis=1, keepdims=True) + EPS)
    mixed_ref[...] = (x_f + acc[0, :, :width]).astype(bf)
    dcs = acc[0, :, width:]
    for k in range(chosen):
        dcomb_ref[:, k : k + 1] = jnp.sum(
            jnp.where(lane == ids_ref[:, k : k + 1], dcs, 0.0), axis=1, keepdims=True
        )
    scaled = acc[1, :, :width] * gain_ref[...]
    dtok_ref[...] = (
        dout_ref[...].astype(f32)
        + inv * scaled
        - x_f * inv * inv * inv * jnp.mean(scaled * x_f, axis=1, keepdims=True)
    ).astype(bf)

    total_gain = dgb[3]
    for k in range(1, G):
        dgz_copy(k).wait_recv()
        total_gain = total_gain + dgb[8 + 2 + k]
    dgain_ref[...] = total_gain

    for a in (0, 1):
        for gg in range(G):
            for up in (True, False):
                edge = g < G - 1 if up else g > 0
                way = gg <= g if up else gg >= g

                @pl.when(jnp.logical_and(edge, way))
                def _():
                    z_copy(a, gg, up).wait_send()

                @pl.when(gg > g if up else gg < g)
                def _():
                    rz_copy(a, up, gg).wait_send()

            p1_copy(a, gg, c).wait_send()
            p2_copy(a, 0, gg, c).wait_send()
            p2_copy(a, 1, gg, first[a]).wait_send()
            q1_copy(a, 0, gg, n1[a]).wait_send()
            q1_copy(a, 1, gg, cxy).wait_send()
            q2_copy(a, gg, n2[a]).wait_send()
            for cc in range(4):
                side_copy(a, gg, cc, s).wait_send()
                rs_copy(a, cc, gg, o).wait_send()
    for k in range(3):
        dg_copy(k).wait_send()
    for k in range(1, G):
        dgz_copy(k).wait_send()
    for store in stores:
        store.wait()


def fused(tokens, norm_gain, combine, expert_ids, w_gate, w_up, w_down, d_out):
    count, width = tokens.shape
    half = w_gate.shape[2]
    G = lax.axis_size("grp")
    devices = lax.axis_size("ctx") * G * lax.axis_size("side")
    total = devices * count
    full = width + LANES
    bf, f32 = jnp.bfloat16, jnp.float32
    vmem = pl.BlockSpec(memory_space=pltpu.VMEM)
    hbm = pl.BlockSpec(memory_space=pl.ANY)
    dma = pltpu.SemaphoreType.DMA
    outs = pl.pallas_call(
        lambda *refs: kernel(G, *refs),
        out_shape=(
            jax.ShapeDtypeStruct(tokens.shape, bf),
            jax.ShapeDtypeStruct(tokens.shape, bf),
            jax.ShapeDtypeStruct((1, width), f32),
            jax.ShapeDtypeStruct(combine.shape, f32),
            jax.ShapeDtypeStruct(w_gate.shape, bf),
            jax.ShapeDtypeStruct(w_up.shape, bf),
            jax.ShapeDtypeStruct(w_down.shape, bf),
        ),
        in_specs=[vmem, vmem, vmem, vmem, hbm, hbm, hbm, vmem],
        out_specs=(vmem, vmem, vmem, vmem, hbm, hbm, hbm),
        scratch_shapes=[
            pltpu.VMEM((devices, count, full), bf),
            pltpu.VMEM((devices, count, full), bf),
            pltpu.VMEM((width, half), bf),
            pltpu.VMEM((width, half), bf),
            pltpu.VMEM((half, width), bf),
            pltpu.VMEM((8, LANES), f32),
            pltpu.VMEM((devices, count, full), bf),
            pltpu.VMEM((devices, count, width), bf),
            pltpu.VMEM((2, devices // 2, count, full), bf),
            pltpu.VMEM((2, 2, G, count, full), bf),
            pltpu.VMEM((2, G, count, full), bf),
            pltpu.VMEM((2, 2, G, count, full), bf),
            pltpu.VMEM((16, 1, width), f32),
            pltpu.VMEM((3, total, half), bf),
            pltpu.VMEM((width, half), bf),
            pltpu.VMEM((width, half), bf),
            pltpu.VMEM((half, width), bf),
            pltpu.VMEM((2, count, full), f32),
            dma((2, 2, G)), dma((2, G)),
            dma((2, G)), dma((2, G)),
            dma((2, 2, G)), dma((2, 2, G)),
            dma((2, 4, G)), dma((2, 4, G)),
            dma((2, 4, G)), dma((2, 4, G)),
            dma((2, 2, G)), dma((2, 2, G)),
            dma((2, G)), dma((2, G)),
            dma((2, 2, G)), dma((2, 2, G)),
            dma((8,)), dma((8,)),
            dma((3,)), dma((3,)),
        ],
        compiler_params=pltpu.CompilerParams(
            collective_id=0, has_side_effects=True, vmem_limit_bytes=60 * 2**20
        ),
    )(tokens, norm_gain[None], combine, expert_ids, w_gate, w_up, w_down, d_out)
    mixed, d_tokens, d_gain, d_combine, g_gate, g_up, g_down = outs
    return mixed, d_tokens, d_gain[0], d_combine, g_gate, g_up, g_down


def solution(mesh):
    in_specs = (
        P(("ctx", "grp", "side"), None),
        P(),
        P(("ctx", "grp", "side"), None),
        P(("ctx", "grp", "side"), None),
        P(("ctx", "grp"), None, "side"),
        P(("ctx", "grp"), None, "side"),
        P(("ctx", "grp"), "side", None),
        P(("ctx", "grp", "side"), None),
    )
    out_specs = (
        P(("ctx", "grp", "side"), None),
        P(("ctx", "grp", "side"), None),
        P(),
        P(("ctx", "grp", "side"), None),
        P(("ctx", "grp"), None, "side"),
        P(("ctx", "grp"), None, "side"),
        P(("ctx", "grp"), "side", None),
    )
    body = fused if fits(mesh) else local
    return jax.shard_map(body, mesh=mesh, in_specs=in_specs, out_specs=out_specs, check_vma=False)
```

```python
import jax
import jax.numpy as jnp
from jax import lax
from jax.experimental import pallas as pl
from jax.experimental.pallas import tpu as pltpu
from jax.sharding import PartitionSpec as P

EPS = 1e-06


def expert_pass(rows, grads, gate_w, up_w, down_w):
    a_gate = jnp.dot(rows, gate_w, preferred_element_type=jnp.float32)
    a_up = jnp.dot(rows, up_w, preferred_element_type=jnp.float32)
    sigmoid_gate = jax.nn.sigmoid(a_gate)
    silu_gate = a_gate * sigmoid_gate
    hidden = (silu_gate * a_up).astype(jnp.bfloat16)
    output = jnp.dot(hidden, down_w, preferred_element_type=jnp.float32)
    d_hidden = lax.dot_general(
        grads, down_w, (((1,), (1,)), ((), ())), preferred_element_type=jnp.float32
    )
    d_up = (d_hidden * silu_gate).astype(jnp.bfloat16)
    d_gate = (d_hidden * a_up * sigmoid_gate * (1.0 + a_gate * (1.0 - sigmoid_gate))).astype(
        jnp.bfloat16
    )
    d_rows = lax.dot_general(
        d_gate, gate_w, (((1,), (1,)), ((), ())), preferred_element_type=jnp.float32
    )
    d_rows = d_rows + lax.dot_general(
        d_up, up_w, (((1,), (1,)), ((), ())), preferred_element_type=jnp.float32
    )
    g_gate = lax.dot_general(
        rows, d_gate, (((0,), (0,)), ((), ())), preferred_element_type=jnp.float32
    )
    g_up = lax.dot_general(rows, d_up, (((0,), (0,)), ((), ())), preferred_element_type=jnp.float32)
    g_down = lax.dot_general(
        hidden, grads, (((0,), (0,)), ((), ())), preferred_element_type=jnp.float32
    )
    return (output, d_rows, g_gate, g_up, g_down)


def local(tokens, norm_gain, combine, expert_ids, w_gate, w_up, w_down, d_out):
    count = tokens.shape[0]
    width = tokens.shape[1]
    chosen = expert_ids.shape[1]
    n_ctx = lax.axis_size("ctx")
    n_grp = lax.axis_size("grp")
    experts = n_ctx * n_grp
    slots = max(2, (4 * count * chosen + 3 * experts - 1) // (3 * experts))
    places = experts * slots
    x_float = tokens.astype(jnp.float32)
    inv_rms = lax.rsqrt(jnp.mean(x_float * x_float, axis=1, keepdims=True) + EPS)
    normed = (x_float * inv_rms * norm_gain).astype(jnp.bfloat16)
    grad_float = d_out.astype(jnp.float32)
    flat_ids = expert_ids.reshape(-1)
    onehot = (flat_ids[:, None] == jnp.arange(experts, dtype=jnp.int32)[None, :]).astype(jnp.int32)
    before = jnp.cumsum(onehot, axis=0) - onehot
    slot = jnp.sum(before * onehot, axis=1)
    target = flat_ids * slots + slot
    select = (target[:, None] == jnp.arange(places, dtype=jnp.int32)[None, :]).astype(jnp.float32)
    per_token = select.reshape(count, chosen, places)
    token_map = jnp.sum(per_token, axis=1).astype(jnp.bfloat16)
    weighted = jnp.sum(per_token * combine[:, :, None], axis=1)
    send_rows = lax.dot_general(
        token_map, normed, (((0,), (0,)), ((), ())), preferred_element_type=jnp.float32
    ).astype(jnp.bfloat16)
    send_grads = lax.dot_general(
        weighted,
        grad_float,
        (((0,), (0,)), ((), ())),
        precision=lax.Precision.HIGHEST,
        preferred_element_type=jnp.float32,
    ).astype(jnp.bfloat16)
    rows_in, grads_in = (
        lax.all_to_all(
            send_rows.reshape(experts, slots, width),
            ("ctx", "grp"),
            split_axis=0,
            concat_axis=0,
            tiled=True,
        ),
        lax.all_to_all(
            send_grads.reshape(experts, slots, width),
            ("ctx", "grp"),
            split_axis=0,
            concat_axis=0,
            tiled=True,
        ),
    )
    full_gate, full_up, full_down = (
        lax.all_gather(w_gate[0], "side", axis=1, tiled=True),
        lax.all_gather(w_up[0], "side", axis=1, tiled=True),
        lax.all_gather(w_down[0], "side", axis=0, tiled=True),
    )
    output, d_rows, g_gate, g_up, g_down = expert_pass(
        rows_in.reshape(places, width),
        grads_in.reshape(places, width),
        full_gate,
        full_up,
        full_down,
    )
    own_gate, own_up, own_down = (
        lax.psum_scatter(g_gate, "side", scatter_dimension=1, tiled=True),
        lax.psum_scatter(g_up, "side", scatter_dimension=1, tiled=True),
        lax.psum_scatter(g_down, "side", scatter_dimension=0, tiled=True),
    )
    back_out = output.astype(jnp.bfloat16)
    back_rows = d_rows.astype(jnp.bfloat16)
    came_out, came_rows = (
        lax.all_to_all(
            back_out.reshape(experts, slots, width),
            ("ctx", "grp"),
            split_axis=0,
            concat_axis=0,
            tiled=True,
        ),
        lax.all_to_all(
            back_rows.reshape(experts, slots, width),
            ("ctx", "grp"),
            split_axis=0,
            concat_axis=0,
            tiled=True,
        ),
    )
    slot_out = jnp.dot(
        select.astype(jnp.bfloat16),
        came_out.reshape(places, width),
        preferred_element_type=jnp.float32,
    ).reshape(count, chosen, width)
    mixed = (x_float + jnp.sum(combine[:, :, None] * slot_out, axis=1)).astype(jnp.bfloat16)
    d_combine = jnp.einsum("tkd,td->tk", slot_out, grad_float, precision=lax.Precision.HIGHEST)
    d_normed = jnp.dot(
        token_map, came_rows.reshape(places, width), preferred_element_type=jnp.float32
    )
    d_gain = lax.psum(jnp.sum(d_normed * x_float * inv_rms, axis=0), ("ctx", "grp", "side"))
    scaled = d_normed * norm_gain
    d_tokens = (
        grad_float
        + inv_rms * scaled
        - x_float * inv_rms**3 * jnp.mean(scaled * x_float, axis=1, keepdims=True)
    )
    return (
        mixed,
        d_tokens.astype(jnp.bfloat16),
        d_gain,
        d_combine,
        own_gate.astype(jnp.bfloat16)[None],
        own_up.astype(jnp.bfloat16)[None],
        own_down.astype(jnp.bfloat16)[None],
    )


MESH = pl.DeviceIdType.MESH
LANES = 128


def fits(mesh):
    return mesh.shape["ctx"] == 4 and mesh.shape["side"] == 2 and mesh.shape["grp"] <= 4


def kernel(
    n_grp,
    tok_ref, gain_ref, comb_ref, ids_ref, wg_hbm, wu_hbm, wd_hbm, dout_ref,
    acc, dgain_ref, gwg, gwu, gwd,
    xg, dg, xs, ds, wg, wu, wd, cw, iw, mo, bo, rs, rp1, rp2, rz, dgb, act,
    zs_s, zs_r, p1_s, p1_r, p2_s, p2_r, sd_s, sd_r,
    rs_s, rs_r, q1_s, q1_r, q2_s, q2_r, rz_s, rz_r, dg_s, dg_r, w_sem,
):
    G = n_grp
    count, width = tok_ref.shape
    full = xg.shape[2]
    half = wg.shape[1]
    chunks = xg.shape[0]
    total = chunks * count
    c, g, s = lax.axis_index("ctx"), lax.axis_index("grp"), lax.axis_index("side")
    x, y = c % 2, c // 2
    cx, cy, cxy = y * 2 + (1 - x), (1 - y) * 2 + x, (1 - y) * 2 + (1 - x)
    o = 1 - s
    expert = c * G + g
    bf, f32 = jnp.bfloat16, jnp.float32

    def idx(cc, gg, ss):
        return (cc * G + gg) * 2 + ss

    def rc(src, dst, ssem, rsem, dev):
        return pltpu.make_async_remote_copy(
            src_ref=src, dst_ref=dst, send_sem=ssem, recv_sem=rsem, device_id=dev, device_id_type=MESH
        )

    loads = [
        pltpu.make_async_copy(a.at[0], b, w_sem.at[i])
        for i, (a, b) in enumerate(((wg_hbm, wg), (wu_hbm, wu), (wd_hbm, wd)))
    ]

    barrier = pltpu.get_barrier_semaphore()
    peers = [(cx, g, s), (cy, g, s), (c, g, o)] + [(c, (g + k) % G, s) for k in range(1, G)]
    for dev in peers:
        pl.semaphore_signal(barrier, inc=1, device_id=dev, device_id_type=MESH)

    x_f = tok_ref[...].astype(f32)
    inv = lax.rsqrt(jnp.mean(x_f * x_f, axis=1, keepdims=True) + EPS)
    table = jnp.zeros((LANES, LANES), f32)
    chosen = ids_ref.shape[0]
    cw[...] = jnp.zeros_like(cw)
    iw[...] = jnp.zeros_like(iw)
    cw[:, :count] = comb_ref[...]
    iw[:, :count] = ids_ref[...]
    row = lax.broadcasted_iota(jnp.int32, (LANES, LANES), 0)
    for k in range(chosen):
        table += jnp.where(row == iw[k : k + 1, :], cw[k : k + 1, :], 0.0)
    table = table.T[:count]
    high = table.astype(bf)
    me = idx(c, g, s)
    xg[me, :, :width] = (x_f * inv * gain_ref[...]).astype(bf)
    xg[me, :, width:] = high
    dg[me, :, :width] = dout_ref[...]
    dg[me, :, width:] = (table - high.astype(f32)).astype(bf)

    pl.semaphore_wait(barrier, len(peers))

    arrays = (xg, dg)
    first, second = (cx, cy), (cy, cx)
    upper = (2 * g) // G

    def place(i):
        return (1 - upper) * (G - 1 - i) + upper * i

    own = place(g)
    far = [place(i + jnp.where(own <= i, 1, 0)) for i in range(G - 1)] + [g]
    near = far[::-1]

    def z_copy(a, gg, up):
        i = idx(c, gg, s)
        to = g + 1 if up else g - 1
        return rc(arrays[a].at[i], arrays[a].at[i], zs_s.at[a, int(up), gg], zs_r.at[a, gg], (c, to, s))

    def p1_copy(a, gg, cc):
        i = idx(cc, gg, s)
        return rc(arrays[a].at[i], arrays[a].at[i], p1_s.at[a, gg], p1_r.at[a, gg], (first[a], g, s))

    def p2_copy(a, j, gg, cc):
        i = idx(cc, gg, s)
        return rc(arrays[a].at[i], arrays[a].at[i], p2_s.at[a, j, gg], p2_r.at[a, j, gg], (second[a], g, s))

    def side_copy(a, gg, cc, ss):
        i = idx(cc, gg, ss)
        return rc(arrays[a].at[i], arrays[a].at[i], sd_s.at[a, cc, gg], sd_r.at[a, cc, gg], (c, g, o))

    def along_z(gg, first_step):
        for a in (0, 1):
            if not first_step:
                z_copy(a, gg, True).wait_recv()

            @pl.when(jnp.logical_and(gg >= g, g > 0))
            def _():
                z_copy(a, gg, False).start()

            @pl.when(jnp.logical_and(gg <= g, g < G - 1))
            def _():
                z_copy(a, gg, True).start()

            p1_copy(a, gg, c).start()
            p2_copy(a, 0, gg, c).start()
            side_copy(a, gg, c, s).start()

    def along_first(gg):
        for a in (0, 1):
            p1_copy(a, gg, first[a]).wait_recv()
            p2_copy(a, 1, gg, first[a]).start()
            side_copy(a, gg, first[a], s).start()

    def along_second(gg):
        for a in (0, 1):
            p2_copy(a, 0, gg, second[a]).wait_recv()
            side_copy(a, gg, second[a], s).start()
        for a in (0, 1):
            p2_copy(a, 1, gg, cxy).wait_recv()
            side_copy(a, gg, cxy, s).start()

    for t in range(G + 2):
        if t < G:
            along_z(near[t], t == 0)
        if t == 0:
            for load in loads:
                load.start()
        if 1 <= t <= G:
            along_first(near[t - 1])
        if t >= 2:
            along_second(near[t - 2])

    for cc in range(4):
        for gg in range(G):
            for a in (0, 1):
                side_copy(a, gg, cc, o).wait_recv()
    for load in loads:
        load.wait()

    per = 2 if G % 2 == 0 else 1
    rows = 8 * per * count
    ch = 8 * per
    mine = (lax.broadcasted_iota(jnp.int32, (rows, LANES), 1) == expert).astype(f32)
    nt = (((1,), (1,)), ((), ()))
    tn = (((0,), (0,)), ((), ()))

    def forward(i, gain_sum):
        places = far[i * per : (i + 1) * per]
        pairs = [(cc, gg) for gg in places for cc in range(4)]

        def fetch(ref, cols):
            parts = [ref[pl.ds(idx(cc, gg, 0), 2), :, cols].reshape(2 * count, -1) for cc, gg in pairs]
            return jnp.concatenate(parts, axis=0)

        def put(ref, cols, value):
            for n, (cc, gg) in enumerate(pairs):
                part = value[n * 2 * count : (n + 1) * 2 * count]
                ref[pl.ds(idx(cc, gg, 0), 2), :, cols] = part.reshape(2, count, -1)

        main, rest = slice(0, width), slice(width, full)
        at = pl.ds(i * rows, rows)
        xr = fetch(xg, main)
        dr = fetch(dg, main)
        xs[at, :] = xr
        ds[at, :] = dr
        weight = fetch(xg, rest).astype(f32) + fetch(dg, rest).astype(f32)
        weight = jnp.sum(weight * mine, axis=1, keepdims=True)
        a_gate = jnp.dot(xr, wg[...], preferred_element_type=f32)
        a_up = jnp.dot(xr, wu[...], preferred_element_type=f32)
        raw = lax.dot_general(dr, wd[...], nt, preferred_element_type=f32)
        sig = jax.nn.sigmoid(a_gate)
        silu = a_gate * sig
        hidden = silu * a_up
        dc = jnp.sum(hidden * raw, axis=1, keepdims=True)
        d_hidden = raw * weight
        hc = (hidden * weight).astype(bf)
        d_up = (d_hidden * silu).astype(bf)
        d_gate = (d_hidden * a_up * sig * (1.0 + a_gate * (1.0 - sig))).astype(bf)
        act[0, at, :] = d_gate
        act[1, at, :] = d_up
        act[2, at, :] = hc
        dcol = jnp.where(weight > 0.0, dc, 0.0) * mine
        put(mo, rest, dcol.astype(bf))
        out = jnp.dot(hc, wd[...], preferred_element_type=f32)
        put(mo, main, out.astype(bf))
        for n, (cc, gg) in enumerate(pairs):
            rs_copy(0, cc, gg, o).start()
        back = lax.dot_general(d_gate, wg[...], nt, preferred_element_type=f32)
        back += lax.dot_general(d_up, wu[...], nt, preferred_element_type=f32)
        put(bo, main, back.astype(bf))
        for n, (cc, gg) in enumerate(pairs):
            rs_copy(1, cc, gg, o).start()
        return gain_sum + jnp.sum(back * xr.astype(f32), axis=0, keepdims=True)

    outs = (mo, bo)
    wide = (full, width)

    def rs_copy(a, cc, gg, ss):
        return rc(
            outs[a].at[idx(cc, gg, ss)], rs.at[a, cc * G + gg, :, : wide[a]],
            rs_s.at[a, cc, gg], rs_r.at[a, cc, gg], (c, g, o),
        )

    n1, n2 = (cy, cx), (cx, cy)

    def q1_copy(a, j, gg, cc):
        return rc(
            outs[a].at[idx(cc, gg, s)], rp1.at[a, j, gg, :, : wide[a]],
            q1_s.at[a, j, gg], q1_r.at[a, j, gg], (n1[a], g, s),
        )

    def q2_copy(a, gg, cc):
        return rc(
            outs[a].at[idx(cc, gg, s)], rp2.at[a, gg, :, : wide[a]],
            q2_s.at[a, gg], q2_r.at[a, gg], (n2[a], g, s),
        )

    def rz_copy(a, up, gg):
        to = g + 1 if up else g - 1
        return rc(
            outs[a].at[idx(c, gg, s)], rz.at[a, int(up), gg, :, : wide[a]],
            rz_s.at[a, int(up), gg], rz_r.at[a, int(up), gg], (c, to, s),
        )

    def add(a, cc, gg, terms):
        i = idx(cc, gg, s)
        value = outs[a][i].astype(f32)
        for term in terms:
            value = value + term[:, : wide[a]].astype(f32)
        outs[a][i] = value.astype(bf)

    gain_sum = jnp.zeros((1, width), f32)
    for i in range(G // per):
        gain_sum = forward(i, gain_sum)
    dgb[0] = gain_sum / gain_ref[...]

    gain_devs = [(c, g, o), (cx, g, s), (cy, g, s)]

    def dg_copy(k):
        return rc(dgb.at[k], dgb.at[8 + k], dg_s.at[k], dg_r.at[k], gain_devs[k])

    def dgz_copy(k):
        return rc(dgb.at[3], dgb.at[8 + 2 + k], dg_s.at[2 + k], dg_r.at[2 + k], (c, (g + k) % G, s))

    dg_copy(0).start()

    def back_first(gg):
        for j, pick in ((1, (cxy, cxy)), (0, n1)):
            for a in (0, 1):
                cc = pick[a]
                rs_copy(a, cc, gg, s).wait_recv()
                add(a, cc, gg, [rs[a, cc * G + gg]])
                q1_copy(a, j, gg, cc).start()

    def back_second(gg):
        for a in (0, 1):
            rs_copy(a, n2[a], gg, s).wait_recv()
            q1_copy(a, 1, gg, cxy).wait_recv()
            add(a, n2[a], gg, [rs[a, n2[a] * G + gg], rp1[a, 1, gg]])
            q2_copy(a, gg, n2[a]).start()

    def back_z(gg):
        for a in (0, 1):
            rs_copy(a, c, gg, s).wait_recv()
            q1_copy(a, 0, gg, c).wait_recv()
            q2_copy(a, gg, c).wait_recv()
            add(a, c, gg, [rs[a, c * G + gg], rp1[a, 0, gg], rp2[a, gg]])
            for up in (True, False):
                @pl.when(gg > g if up else gg < g)
                def _():
                    @pl.when(g > 0 if up else g < G - 1)
                    def _():
                        rz_copy(a, up, gg).wait_recv()
                        add(a, c, gg, [rz[a, int(up), gg]])

                    rz_copy(a, up, gg).start()

    blocks = 8
    blk = width // blocks

    def grads(i):
        cols = slice(i * blk, (i + 1) * blk)
        xr = xs[:, cols]
        dr = ds[:, cols]
        gwg[0, cols, :] = lax.dot_general(xr, act[0], tn, preferred_element_type=f32).astype(bf)
        gwu[0, cols, :] = lax.dot_general(xr, act[1], tn, preferred_element_type=f32).astype(bf)
        gwd[0, :, cols] = lax.dot_general(act[2], dr, tn, preferred_element_type=f32).astype(bf)

    todo = list(range(blocks))
    for t in range(G + 3):
        if t < G:
            back_first(far[t])
        if t == 1:
            dg_copy(0).wait_recv()
            dgb[1] = dgb[0] + dgb[8]
            dg_copy(1).start()
        if t == 3:
            dg_copy(1).wait_recv()
            dgb[2] = dgb[1] + dgb[9]
            dg_copy(2).start()
        if t == 5:
            dg_copy(2).wait_recv()
            dgb[3] = dgb[2] + dgb[10]
            for k in range(1, G):
                dgz_copy(k).start()
        if 2 <= t < G + 2:
            back_second(far[t - 2])
        if t >= 3:
            back_z(far[t - 3])
        for _ in range(2 if t in (1, G - 1, G) else 1):
            if todo and t >= 1:
                grads(todo.pop(0))
    for i in todo:
        grads(i)

    for a in (0, 1):
        acc[a, :, : wide[a]] = outs[a][me].astype(f32)
        for up in (True, False):
            @pl.when(g > 0 if up else g < G - 1)
            def _():
                rz_copy(a, up, g).wait_recv()
                acc[a, :, : wide[a]] += rz[a, int(up), g, :, : wide[a]].astype(f32)
    acc[1, :, width:] = jnp.zeros((count, LANES), f32)

    total_gain = dgb[3]
    for k in range(1, G):
        dgz_copy(k).wait_recv()
        total_gain = total_gain + dgb[8 + 2 + k]
    dgain_ref[...] = total_gain

    for a in (0, 1):
        for gg in range(G):
            for up in (True, False):
                edge = g < G - 1 if up else g > 0
                way = gg <= g if up else gg >= g

                @pl.when(jnp.logical_and(edge, way))
                def _():
                    z_copy(a, gg, up).wait_send()

                @pl.when(gg > g if up else gg < g)
                def _():
                    rz_copy(a, up, gg).wait_send()

            p1_copy(a, gg, c).wait_send()
            p2_copy(a, 0, gg, c).wait_send()
            p2_copy(a, 1, gg, first[a]).wait_send()
            q1_copy(a, 0, gg, n1[a]).wait_send()
            q1_copy(a, 1, gg, cxy).wait_send()
            q2_copy(a, gg, n2[a]).wait_send()
            for cc in range(4):
                side_copy(a, gg, cc, s).wait_send()
                rs_copy(a, cc, gg, o).wait_send()
    for k in range(3):
        dg_copy(k).wait_send()
    for k in range(1, G):
        dgz_copy(k).wait_send()


def finish(
    acc, gain_sum, gwg, gwu, gwd, tok_ref, gain_ref, ids_ref, dout_ref,
    mixed_ref, dtok_ref, dgain_ref, dcomb_ref, gg_hbm, gu_hbm, gd_hbm, iw, sem,
):
    stores = [
        pltpu.make_async_copy(b, a, sem.at[i])
        for i, (a, b) in enumerate(((gg_hbm, gwg), (gu_hbm, gwu), (gd_hbm, gwd)))
    ]
    for store in stores:
        store.start()
    bf, f32 = jnp.bfloat16, jnp.float32
    count, width = tok_ref.shape
    x_f = tok_ref[...].astype(f32)
    inv = lax.rsqrt(jnp.mean(x_f * x_f, axis=1, keepdims=True) + EPS)
    mixed_ref[...] = (x_f + acc[0, :, :width]).astype(bf)
    iw[...] = jnp.zeros_like(iw)
    iw[:, :count] = ids_ref[...]
    row = lax.broadcasted_iota(jnp.int32, (LANES, LANES), 0)
    dcs = jnp.concatenate([acc[0, :, width:], jnp.zeros((LANES - count, LANES), f32)], axis=0).T
    for k in range(ids_ref.shape[0]):
        got = jnp.sum(jnp.where(row == iw[k : k + 1, :], dcs, 0.0), axis=0, keepdims=True)
        dcomb_ref[k : k + 1, :] = got[:, :count]
    scaled = acc[1, :, :width] * gain_ref[...]
    dtok_ref[...] = (
        dout_ref[...].astype(f32)
        + inv * scaled
        - x_f * inv * inv * inv * jnp.mean(scaled * x_f, axis=1, keepdims=True)
    ).astype(bf)
    dgain_ref[...] = gain_sum[...]
    for store in stores:
        store.wait()


def fused(tokens, norm_gain, combine, expert_ids, w_gate, w_up, w_down, d_out):
    count, width = tokens.shape
    half = w_gate.shape[2]
    G = lax.axis_size("grp")
    devices = lax.axis_size("ctx") * G * lax.axis_size("side")
    total = devices * count
    full = width + LANES
    bf, f32 = jnp.bfloat16, jnp.float32
    vmem = pl.BlockSpec(memory_space=pltpu.VMEM)
    hbm = pl.BlockSpec(memory_space=pl.ANY)
    dma = pltpu.SemaphoreType.DMA
    gain = norm_gain[None]
    combine_t, ids_t = combine.T, expert_ids.T
    ids_pad = (combine.shape[1], LANES)
    acc, gain_sum, g_gate, g_up, g_down = pl.pallas_call(
        lambda *refs: kernel(G, *refs),
        out_shape=(
            jax.ShapeDtypeStruct((2, count, full), f32),
            jax.ShapeDtypeStruct((1, width), f32),
            jax.ShapeDtypeStruct(w_gate.shape, bf),
            jax.ShapeDtypeStruct(w_up.shape, bf),
            jax.ShapeDtypeStruct(w_down.shape, bf),
        ),
        in_specs=[vmem, vmem, vmem, vmem, hbm, hbm, hbm, vmem],
        out_specs=(vmem,) * 5,
        scratch_shapes=[
            pltpu.VMEM((devices, count, full), bf),
            pltpu.VMEM((devices, count, full), bf),
            pltpu.VMEM((total, width), bf),
            pltpu.VMEM((total, width), bf),
            pltpu.VMEM((width, half), bf),
            pltpu.VMEM((width, half), bf),
            pltpu.VMEM((half, width), bf),
            pltpu.VMEM(ids_pad, f32),
            pltpu.VMEM(ids_pad, jnp.int32),
            pltpu.VMEM((devices, count, full), bf),
            pltpu.VMEM((devices, count, width), bf),
            pltpu.VMEM((2, devices // 2, count, full), bf),
            pltpu.VMEM((2, 2, G, count, full), bf),
            pltpu.VMEM((2, G, count, full), bf),
            pltpu.VMEM((2, 2, G, count, full), bf),
            pltpu.VMEM((16, 1, width), f32),
            pltpu.VMEM((3, total, half), bf),
            dma((2, 2, G)), dma((2, G)),
            dma((2, G)), dma((2, G)),
            dma((2, 2, G)), dma((2, 2, G)),
            dma((2, 4, G)), dma((2, 4, G)),
            dma((2, 4, G)), dma((2, 4, G)),
            dma((2, 2, G)), dma((2, 2, G)),
            dma((2, G)), dma((2, G)),
            dma((2, 2, G)), dma((2, 2, G)),
            dma((8,)), dma((8,)),
            dma((3,)),
        ],
        compiler_params=pltpu.CompilerParams(
            collective_id=0, has_side_effects=True, vmem_limit_bytes=46 * 2**20
        ),
    )(tokens, gain, combine_t, ids_t, w_gate, w_up, w_down, d_out)
    mixed, d_tokens, d_gain, d_combine, g_gate, g_up, g_down = pl.pallas_call(
        finish,
        out_shape=(
            jax.ShapeDtypeStruct(tokens.shape, bf),
            jax.ShapeDtypeStruct(tokens.shape, bf),
            jax.ShapeDtypeStruct((1, width), f32),
            jax.ShapeDtypeStruct(combine_t.shape, f32),
            jax.ShapeDtypeStruct(w_gate.shape, bf),
            jax.ShapeDtypeStruct(w_up.shape, bf),
            jax.ShapeDtypeStruct(w_down.shape, bf),
        ),
        in_specs=[vmem] * 9,
        out_specs=(vmem,) * 4 + (hbm,) * 3,
        scratch_shapes=[pltpu.VMEM(ids_pad, jnp.int32), dma((3,))],
        compiler_params=pltpu.CompilerParams(vmem_limit_bytes=12 * 2**20),
    )(acc, gain_sum, g_gate, g_up, g_down, tokens, gain, ids_t, d_out)
    return mixed, d_tokens, d_gain[0], d_combine.T, g_gate, g_up, g_down


def solution(mesh):
    in_specs = (
        P(("ctx", "grp", "side"), None),
        P(),
        P(("ctx", "grp", "side"), None),
        P(("ctx", "grp", "side"), None),
        P(("ctx", "grp"), None, "side"),
        P(("ctx", "grp"), None, "side"),
        P(("ctx", "grp"), "side", None),
        P(("ctx", "grp", "side"), None),
    )
    out_specs = (
        P(("ctx", "grp", "side"), None),
        P(("ctx", "grp", "side"), None),
        P(),
        P(("ctx", "grp", "side"), None),
        P(("ctx", "grp"), None, "side"),
        P(("ctx", "grp"), None, "side"),
        P(("ctx", "grp"), "side", None),
    )
    body = fused if fits(mesh) else local
    return jax.shard_map(body, mesh=mesh, in_specs=in_specs, out_specs=out_specs, check_vma=False)
```
